32 devices in a mesh: cp: 8 (over z, x), tp: 4 (over y, core).
Axes of the slice: x: 2, y: 2, z: 4, core: 2. Of those that a mesh axis runs over, the one named last changes fastest.
Arguments:
- tokens: bfloat16 [4096, 4096], P(('cp', 'tp')), may hold values from -6 to 6
- grad_out: bfloat16 [4096, 4096], P(('cp', 'tp')), may hold values from -6 to 6
- expert_ids: int32 [4096, 1], P(('cp', 'tp')), may hold values from 0 to 7; in each aligned block of 128 rows (0 to 127, 128 to 255, ...) at most 24 rows name the same one
- router_weights: float32 [4096, 1], P(('cp', 'tp')), may hold values from 0.2 to 1
- gate_weight: bfloat16 [8, 1536, 4096], P('cp', 'tp'), may hold values from -0.09375 to 0.09375
- up_weight: bfloat16 [8, 1536, 4096], P('cp', 'tp'), may hold values from -0.09375 to 0.09375
- down_weight: bfloat16 [8, 1536, 4096], P('cp', 'tp'), may hold values from -0.15625 to 0.15625
Outputs:
- grad_tokens: bfloat16 [4096, 4096], P(('cp', 'tp'))
- grad_gate: float32 [8, 1536, 4096], P('cp', 'tp')
- grad_up: float32 [8, 1536, 4096], P('cp', 'tp')
- grad_down: float32 [8, 1536, 4096], P('cp', 'tp')
The draws below stay inside these ranges and needn't reach their ends.
Inputs may be any that keep to these rules, and one draw needn't show every extreme that they name: `expert_ids`: within each aligned block of 128 consecutive rows (rows 0 to 127, 128 to 255, and so on) each expert is named at most 24 times, and in some block some expert is named exactly 24 times.
All inputs are finite; a program needn't handle non-finite values.
Results may differ from the reference program's by a relative error of at most 0.009.
Values may be sent and summed in bfloat16 or wider, within the bound.
A program may use at most 256 MiB of HBM per device.

```python
import math
import jax
import jax.numpy as jnp
import numpy as np
from jax import lax

D = 4096
FF = 1536
TOK_DEV = 128
TOP = 1
EXPERTS = 8
CAP = 24
TOKENS = 4096
N_CP = 8
N_TP = 4


def steps_of(key, extent, split, smallest, top_value):
    def one(position, blocks):
        steps = jax.random.uniform(jax.random.fold_in(jax.random.fold_in(key, 6), position), (blocks,), jnp.float32, smallest / len(split), top_value / len(split))
        return jnp.repeat(jnp.exp(steps), extent[position] // blocks).reshape((-1,) + (1,) * (len(extent) - position - 1))

    level = one(*split[0])
    for cut in split[1:]:
        level = level * one(*cut)
    return level


def shared_out(key, own, number, rows, amount, top, reach, skew):
    sequence = jax.random.permutation(key, amount)
    heavy_load, ordinary = portions_of(amount, rows * top, reach, skew, True), portions_of(amount, rows * top, reach, skew, False)
    places = jnp.arange(amount)

    def named(lengths, turn):
        used = int((lengths > 0).sum())
        fixed = max(1, used // 4)
        passed = fixed + (places - fixed + turn * (used - fixed)) % max(1, amount - fixed)
        return jnp.zeros((amount,), jnp.int32).at[sequence[jnp.where(places < fixed, places, passed)]].set(jnp.asarray(lengths, jnp.int32))

    lengths = jnp.where(number % 4 == 0, named(heavy_load, number // 4), named(ordinary, number - number // 4 - 1))
    mixed = jax.random.permutation(jax.random.fold_in(own, 3), amount)
    giver, sink = mixed[0:amount // 2 * 2:2], mixed[1:amount // 2 * 2:2]
    margin = jnp.minimum(lengths[giver] - 1, reach - lengths[sink]) // 2
    margin = jnp.where((giver == sequence[0]) | (sink == sequence[0]) | (lengths[sink] == 0), 0, jnp.maximum(margin, 0))
    passed = jax.random.randint(jax.random.fold_in(own, 4), (amount // 2,), 0, 1 << 20) % (margin + 1)
    lengths = lengths.at[giver].add(-passed).at[sink].add(passed)
    items = jnp.searchsorted(jnp.cumsum(lengths), jnp.arange(rows * top), side="right").astype(jnp.int32)
    table = items.reshape(top, rows).T
    table = table[jax.random.permutation(jax.random.fold_in(own, 1), rows)]
    turn = jax.random.randint(jax.random.fold_in(own, 2), (rows, 1), 0, top)
    return jnp.take_along_axis(table, (jnp.arange(top)[None, :] + turn) % top, axis=1)


def portions_of(amount, total, bound, skew, full):
    loads = [(1 << 20) // math.isqrt(rank ** skew) + 1 for rank in range(1, amount + 1)]
    largest = bound if full else min(bound, max(-(-total // amount), total * loads[0] // sum(loads)))
    least = 1 if total - largest >= amount - 1 else 0
    holding, spare = [largest] + [least] * (amount - 1), total - largest - least * (amount - 1)
    while spare > 0:
        candidates = [i for i in range(1, amount) if holding[i] < largest] or [i for i in range(1, amount) if holding[i] < bound]
        pool, left = sum([loads[i] for i in candidates]), spare
        for i in candidates:
            more = min(bound - holding[i], max(1, left * loads[i] // pool), spare)
            holding[i] = holding[i] + more
            spare = spare - more
    return np.array(holding)


def noise(rng, extent, width, bound, split=(), kind=jnp.bfloat16):
    factor_of = steps_of(rng, extent, split, -0.22, 0.18) if split else 1.0
    entries = jax.random.normal(rng, extent, jnp.float32) * width * factor_of
    return jnp.minimum(jnp.maximum(entries, -bound), bound).astype(kind)


def setup_inputs(seed: int = 0) -> dict:
    arg_keys = jax.random.split(jax.random.key(seed), 8)
    tokens = noise(arg_keys[0], (TOKENS, D), 1.0, 6.0, ((0, 32),))
    grad_out = noise(arg_keys[1], (TOKENS, D), 1.0, 6.0, ((0, 32),))
    expert_ids_keys = jax.random.split(jax.random.fold_in(arg_keys[2], 1), TOKENS // TOK_DEV)
    expert_ids_turns = jax.random.permutation(jax.random.fold_in(arg_keys[2], 3), TOKENS // TOK_DEV)
    expert_ids = jax.vmap(lambda own, number: shared_out(jax.random.fold_in(arg_keys[2], 2), own, number, TOK_DEV, EXPERTS, TOP, CAP, 1))(expert_ids_keys, expert_ids_turns).reshape((TOKENS, TOP))
    router_weights = jnp.clip(0.2 + 0.8 * jax.random.uniform(arg_keys[3], (TOKENS, TOP), jnp.float32) ** steps_of(arg_keys[3], (TOKENS, TOP), ((0, 32),), -0.2, 0.2), 0.2, 1.0)
    gate_weight = noise(arg_keys[4], (EXPERTS, FF, D), D ** -0.5, 0.09375, ((0, 8), (1, 4)))
    up_weight = noise(arg_keys[5], (EXPERTS, FF, D), D ** -0.5, 0.09375, ((0, 8), (1, 4)))
    down_weight = noise(arg_keys[6], (EXPERTS, FF, D), FF ** -0.5, 0.15625, ((0, 8), (1, 4)))
    return dict(tokens=tokens, grad_out=grad_out, expert_ids=expert_ids, router_weights=router_weights, gate_weight=gate_weight, up_weight=up_weight, down_weight=down_weight)


def reference(tokens, grad_out, expert_ids, router_weights, gate_weight, up_weight, down_weight):
    ndev = N_CP * N_TP
    per_dev = TOK_DEV * TOP
    ids = expert_ids.reshape(ndev, per_dev).astype(jnp.int32)
    onehot = (ids[:, :, None] == jnp.arange(EXPERTS, dtype=jnp.int32)[None, None, :]).astype(jnp.int32)
    before = jnp.cumsum(onehot, axis=1) - onehot
    rank = jnp.sum(before * onehot, axis=2)
    place = jnp.arange(ndev, dtype=jnp.int32)[:, None] * CAP + rank
    flat_ids = ids.reshape(-1)
    flat_place = place.reshape(-1).astype(jnp.int32)
    owner = jnp.full((EXPERTS, ndev * CAP), -1, jnp.int32)
    owner = owner.at[flat_ids, flat_place].set(jnp.arange(TOKENS * TOP, dtype=jnp.int32))
    x_assign = jnp.repeat(tokens, TOP, axis=0)
    g_assign = (router_weights.reshape(-1, 1) * jnp.repeat(grad_out, TOP, axis=0).astype(jnp.float32)).astype(jnp.bfloat16)
    block = FF // N_TP

    def expert(args):
        index_row, w_gate, w_up, w_down = args
        valid = (index_row >= 0)[:, None]
        safe = jnp.maximum(index_row, 0)
        slot_in = jnp.where(valid, x_assign[safe].astype(jnp.float32), jnp.float32(0.0))
        slot_go = jnp.where(valid, g_assign[safe].astype(jnp.float32), jnp.float32(0.0))
        wg32 = w_gate.astype(jnp.float32)
        wu32 = w_up.astype(jnp.float32)
        wd32 = w_down.astype(jnp.float32)
        gate = jnp.dot(slot_in, wg32.T, preferred_element_type=jnp.float32)
        upval = jnp.dot(slot_in, wu32.T, preferred_element_type=jnp.float32)
        sig = jax.nn.sigmoid(gate)
        act = gate * sig
        hidden = lax.optimization_barrier((act * upval).astype(jnp.bfloat16)).astype(jnp.float32)
        grad_hidden = jnp.dot(slot_go, wd32.T, preferred_element_type=jnp.float32)
        grad_upin = lax.optimization_barrier((grad_hidden * act).astype(jnp.bfloat16)).astype(jnp.float32)
        grad_gatein = lax.optimization_barrier((grad_hidden * upval * sig * (1.0 + gate * (1.0 - sig))).astype(jnp.bfloat16)).astype(jnp.float32)
        grad_down = jnp.dot(hidden.T, slot_go, preferred_element_type=jnp.float32)
        grad_gate = jnp.dot(grad_gatein.T, slot_in, preferred_element_type=jnp.float32)
        grad_up = jnp.dot(grad_upin.T, slot_in, preferred_element_type=jnp.float32)
        total = jnp.zeros(slot_in.shape, jnp.float32)
        for which in range(N_TP):
            lo = which * block
            hi = lo + block
            part = jnp.dot(grad_gatein[:, lo:hi], wg32[lo:hi], preferred_element_type=jnp.float32)
            part = part + jnp.dot(grad_upin[:, lo:hi], wu32[lo:hi], preferred_element_type=jnp.float32)
            total = total + lax.optimization_barrier(part.astype(jnp.bfloat16)).astype(jnp.float32)
        return total.astype(jnp.bfloat16), grad_gate, grad_up, grad_down

    slot_grads, grad_gate, grad_up, grad_down = lax.map(expert, (owner, gate_weight, up_weight, down_weight))
    per_pick = slot_grads[flat_ids, flat_place].astype(jnp.float32)
    grad_tokens = jnp.sum(per_pick.reshape(TOKENS, TOP, D), axis=1).astype(jnp.bfloat16)
    return grad_tokens, grad_gate, grad_up, grad_down
```

```python
import functools

import jax
import jax.numpy as jnp
from jax import lax
from jax.experimental import pallas as pl
from jax.experimental.pallas import tpu as pltpu
from jax.sharding import PartitionSpec as P

F32 = jnp.float32
BF16 = jnp.bfloat16
ROWS_LAST = (((1,), (1,)), ((), ()))
ROWS_FIRST = (((0,), (0,)), ((), ()))


def flip(c, d, n):
    total, b = 0, 1
    while b < n:
        bit = (c // b) % 2
        total = total + ((1 - bit) if d & b else bit) * b
        b *= 2
    return total


def positions(n_tp):
    c = lax.axis_index("cp")
    t = lax.axis_index("tp")
    n_y = n_tp // 2
    k = t % 2
    y = t // 2
    return c, t, n_y, k, y


def greet(n_cp, n_tp):
    c, t, n_y, k, y = positions(n_tp)
    barrier = pltpu.get_barrier_semaphore()
    peers = [(flip(c, d, n_cp), t) for d in range(1, n_cp)]
    peers += [(c, ((y + dy) % n_y) * 2 + k) for dy in range(1, n_y)]
    peers += [(c, y * 2 + 1 - k)]
    for peer in peers:
        pl.semaphore_signal(barrier, inc=1, device_id=peer, device_id_type=pl.DeviceIdType.MESH)
    pl.semaphore_wait(barrier, len(peers))


def remote(src, dst, send, recv, peer):
    return pltpu.make_async_remote_copy(
        src_ref=src, dst_ref=dst, send_sem=send, recv_sem=recv,
        device_id=peer, device_id_type=pl.DeviceIdType.MESH,
    )


def send_order(n_cp):
    far = list(range(n_cp // 2, n_cp))
    near = list(range(1, n_cp // 2))
    out = []
    for i, f in enumerate(far):
        out.append(f)
        if i < len(near):
            out.append(near[i])
    return out


def dispatch_kernel(n_cp, n_tp, xg, out, loc, cp_s, cp_r, y_s, y_r, s_s, s_r, f_s, f_r):
    c, t, n_y, k, y = positions(n_tp)
    sib = y * 2 + 1 - k
    greet(n_cp, n_tp)

    def cell(s, tt):
        return out.at[:, s * n_tp + tt]

    def cp_copy(d):
        peer = flip(c, d, n_cp)
        return remote(xg.at[:, peer], cell(c, t), cp_s.at[d], cp_r.at[d], (peer, t))

    def have(d):
        return xg.at[:, c] if d == 0 else cell(flip(c, d, n_cp), t)

    def y_copy(d, dy):
        to = ((y + dy) % n_y) * 2 + k
        return remote(have(d), cell(flip(c, d, n_cp), t), y_s.at[d, dy], y_r.at[d, dy], (c, to))

    def s_copy(d):
        return remote(have(d), cell(flip(c, d, n_cp), t), s_s.at[d], s_r.at[d], (c, sib))

    def f_copy(d, dy):
        part = cell(flip(c, d, n_cp), ((y + n_y - dy) % n_y) * 2 + k)
        return remote(part, part, f_s.at[d, dy], f_r.at[d, dy], (c, sib))

    own = pltpu.make_async_copy(xg.at[:, c], cell(c, t), loc)
    own.start()
    for d in send_order(n_cp):
        cp_copy(d).start()
    order = list(range(n_cp))
    for i in range(n_cp + 1):
        if i < n_cp:
            d = order[i]
            if d:
                cp_copy(d).wait_recv()
            for dy in range(1, n_y):
                y_copy(d, dy).start()
            s_copy(d).start()
        if i > 0:
            d = order[i - 1]
            for dy in range(1, n_y):
                y_copy(d, dy).wait_recv()
                f_copy(d, dy).start()
    own.wait()
    for d in range(n_cp):
        if d:
            cp_copy(d).wait_send()
        for dy in range(1, n_y):
            y_copy(d, dy).wait_send()
            f_copy(d, dy).wait()
        s_copy(d).wait()


def return_kernel(n_cp, n_tp, p, out, a, sb, yb, tb, loc, s_s, s_r, y_s, y_r, cp_s, cp_r):
    c, t, n_y, k, y = positions(n_tp)
    sib = y * 2 + 1 - k
    greet(n_cp, n_tp)
    order = list(range(n_cp // 2, n_cp)) + list(range(n_cp // 2))

    def s_copy(d, yy):
        s = flip(c, d, n_cp)
        return remote(
            p.at[s * n_tp + yy * 2 + 1 - k], a.at[d * n_y + yy],
            s_s.at[d, yy], s_r.at[d, yy], (c, sib),
        )

    def y_copy(d, dy):
        to = ((y + dy) % n_y) * 2 + k
        return remote(sb.at[d, dy], yb.at[d, dy], y_s.at[d, dy], y_r.at[d, dy], (c, to))

    def cp_copy(d):
        peer = flip(c, d, n_cp)
        return remote(tb.at[d], out.at[c], cp_s.at[d], cp_r.at[d], (peer, t))

    def pair(d, yy):
        s = flip(c, d, n_cp)
        return p[s * n_tp + yy * 2 + k].astype(F32) + a[d * n_y + yy].astype(F32)

    for d in order:
        for yy in range(n_y):
            s_copy(d, yy).start()
    own = pltpu.make_async_copy(tb.at[0], out.at[c], loc)
    for i in range(n_cp + 1):
        if i < n_cp:
            d = order[i]
            for yy in range(n_y):
                s_copy(d, yy).wait_recv()
            for dy in range(1, n_y):
                sb[d, dy] = pair(d, (y + dy) % n_y).astype(BF16)
                y_copy(d, dy).start()
        if i > 0:
            d = order[i - 1]
            total = pair(d, y)
            for dy in range(1, n_y):
                y_copy(d, dy).wait_recv()
                total = total + yb[d, dy].astype(F32)
            tb[d] = total.astype(BF16)
            if d:
                cp_copy(d).start()
            else:
                own.start()
    own.wait()
    for d in range(n_cp):
        for yy in range(n_y):
            s_copy(d, yy).wait_send()
        for dy in range(1, n_y):
            y_copy(d, dy).wait_send()
        if d:
            cp_copy(d).wait()


def dispatch(xg, n_cp, n_tp):
    _, _, slots, width = xg.shape
    n_y = n_tp // 2
    dma = pltpu.SemaphoreType.DMA
    return pl.pallas_call(
        functools.partial(dispatch_kernel, n_cp, n_tp),
        out_shape=jax.ShapeDtypeStruct((2, n_cp * n_tp, slots, width), BF16),
        in_specs=[pl.BlockSpec(memory_space=pl.ANY)],
        out_specs=pl.BlockSpec(memory_space=pl.ANY),
        scratch_shapes=[
            dma, dma((n_cp,)), dma((n_cp,)), dma((n_cp, n_y)), dma((n_cp, n_y)),
            dma((n_cp,)), dma((n_cp,)), dma((n_cp, n_y)), dma((n_cp, n_y)),
        ],
        compiler_params=pltpu.CompilerParams(collective_id=0, has_side_effects=True),
        name="dispatch",
    )(xg)


def give_back(p, n_cp, n_tp):
    _, slots, width = p.shape
    n_y = n_tp // 2
    dma = pltpu.SemaphoreType.DMA
    return pl.pallas_call(
        functools.partial(return_kernel, n_cp, n_tp),
        out_shape=jax.ShapeDtypeStruct((n_cp, slots, width), BF16),
        in_specs=[pl.BlockSpec(memory_space=pltpu.VMEM)],
        out_specs=pl.BlockSpec(memory_space=pltpu.VMEM),
        scratch_shapes=[
            pltpu.VMEM((n_cp * n_y, slots, width), BF16),
            pltpu.VMEM((n_cp, n_y, slots, width), BF16),
            pltpu.VMEM((n_cp, n_y, slots, width), BF16),
            pltpu.VMEM((n_cp, slots, width), BF16),
            dma, dma((n_cp, n_y)), dma((n_cp, n_y)), dma((n_cp, n_y)), dma((n_cp, n_y)),
            dma((n_cp,)), dma((n_cp,)),
        ],
        compiler_params=pltpu.CompilerParams(
            collective_id=1, has_side_effects=True, vmem_limit_bytes=56 << 20
        ),
        name="give_back",
    )(p)


def body(tokens, grad_out, expert_ids, router_weights, gate_weight, up_weight, down_weight):
    n_cp = lax.axis_size("cp")
    n_tp = lax.axis_size("tp")
    tok_rows, width = tokens.shape
    picks = expert_ids.shape[1]
    count = tok_rows * picks
    slots = -(-max(2, 3 * tok_rows * picks // (2 * n_cp)) // 8) * 8
    flat_ids = expert_ids.reshape(count)
    onehot = (flat_ids[:, None] == jnp.arange(n_cp, dtype=jnp.int32)[None, :]).astype(jnp.int32)
    before = jnp.cumsum(onehot, axis=0) - onehot
    rank = jnp.sum(before * onehot, axis=1)
    place = flat_ids * slots + rank
    placer = (place[None, :] == jnp.arange(n_cp * slots, dtype=jnp.int32)[:, None]).astype(BF16)
    x_assign = jnp.repeat(tokens, picks, axis=0)
    g_assign = (router_weights.reshape(count, 1) * jnp.repeat(grad_out, picks, axis=0).astype(F32)).astype(BF16)
    xg = jnp.stack([
        jnp.dot(placer, x_assign, preferred_element_type=F32).astype(BF16),
        jnp.dot(placer, g_assign, preferred_element_type=F32).astype(BF16),
    ]).reshape(2, n_cp, slots, width)
    w_gate = gate_weight[0]
    w_up = up_weight[0]
    w_down = down_weight[0]
    got = dispatch(xg, n_cp, n_tp).reshape(2, n_cp * n_tp * slots, width)
    slot_in, slot_go = got[0], got[1]
    gate = lax.dot_general(slot_in, w_gate, ROWS_LAST, preferred_element_type=F32)
    upval = lax.dot_general(slot_in, w_up, ROWS_LAST, preferred_element_type=F32)
    sig = jax.nn.sigmoid(gate)
    act = gate * sig
    hidden = (act * upval).astype(BF16)
    grad_hidden = lax.dot_general(slot_go, w_down, ROWS_LAST, preferred_element_type=F32)
    grad_upin = (grad_hidden * act).astype(BF16)
    grad_gatein = (grad_hidden * upval * sig * (1.0 + gate * (1.0 - sig))).astype(BF16)
    part = jnp.dot(grad_gatein, w_gate, preferred_element_type=F32)
    part = part + jnp.dot(grad_upin, w_up, preferred_element_type=F32)
    slot_grad = give_back(part.astype(BF16).reshape(n_cp * n_tp, slots, width), n_cp, n_tp)
    grad_down = lax.dot_general(hidden, slot_go, ROWS_FIRST, preferred_element_type=F32)
    grad_gate = lax.dot_general(grad_gatein, slot_in, ROWS_FIRST, preferred_element_type=F32)
    grad_up = lax.dot_general(grad_upin, slot_in, ROWS_FIRST, preferred_element_type=F32)
    pick_grad = lax.dot_general(
        placer, slot_grad.reshape(n_cp * slots, width), ROWS_FIRST, preferred_element_type=F32
    )
    grad_tokens = jnp.sum(pick_grad.reshape(tok_rows, picks, width), axis=1).astype(BF16)
    return (grad_tokens, grad_gate[None], grad_up[None], grad_down[None])


def solution(mesh):
    tok = P(("cp", "tp"), None)
    wgt = P("cp", "tp", None)
    return jax.shard_map(
        body,
        mesh=mesh,
        in_specs=(tok, tok, tok, tok, wgt, wgt, wgt),
        out_specs=(tok, wgt, wgt, wgt),
        check_vma=False,
    )
```

```python
import functools

import jax
import jax.numpy as jnp
from jax import lax
from jax.experimental import pallas as pl
from jax.experimental.pallas import tpu as pltpu
from jax.sharding import PartitionSpec as P

F32 = jnp.float32
BF16 = jnp.bfloat16
ROWS_LAST = (((1,), (1,)), ((), ()))
ROWS_FIRST = (((0,), (0,)), ((), ()))


def flip(c, d, n):
    total, b = 0, 1
    while b < n:
        bit = (c // b) % 2
        total = total + ((1 - bit) if d & b else bit) * b
        b *= 2
    return total


def positions(n_tp):
    c = lax.axis_index("cp")
    t = lax.axis_index("tp")
    n_y = n_tp // 2
    k = t % 2
    y = t // 2
    return c, t, n_y, k, y


def greet(n_cp, n_tp):
    c, t, n_y, k, y = positions(n_tp)
    barrier = pltpu.get_barrier_semaphore()
    peers = [(flip(c, d, n_cp), t) for d in range(1, n_cp)]
    peers += [(c, ((y + dy) % n_y) * 2 + k) for dy in range(1, n_y)]
    peers += [(c, y * 2 + 1 - k)]
    for peer in peers:
        pl.semaphore_signal(barrier, inc=1, device_id=peer, device_id_type=pl.DeviceIdType.MESH)
    pl.semaphore_wait(barrier, len(peers))


def remote(src, dst, send, recv, peer):
    return pltpu.make_async_remote_copy(
        src_ref=src, dst_ref=dst, send_sem=send, recv_sem=recv,
        device_id=peer, device_id_type=pl.DeviceIdType.MESH,
    )


DEPTH = 1


def process_order(n_cp):
    far = list(range(n_cp // 2, n_cp))
    near = list(range(1, n_cp // 2))
    out = [0]
    for i, f in enumerate(far):
        if i < len(near):
            out.append(near[i])
        if f == far[-1]:
            out.append(None)
        out.append(f)
    return out


def fused_kernel(
    n_cp, n_tp, slots,
    xg, wg_h, wu_h, wd_h,
    got, hid_o, gg_o, gu_o, out,
    wg, wu, wd, buf, p, a, sb, yb, tb,
    loc, w_sem, l_sem, cp_s, cp_r, y_s, y_r, s_s, s_r, f_s, f_r,
    rs_s, rs_r, ry_s, ry_r, rc_s, rc_r,
):
    c, t, n_y, k, y = positions(n_tp)
    sib = y * 2 + 1 - k
    rows = n_tp * slots
    width = xg.shape[-1]

    loads = [
        pltpu.make_async_copy(h, v, w_sem.at[i])
        for i, (h, v) in enumerate(((wg_h, wg), (wu_h, wu), (wd_h, wd)))
    ]
    greet(n_cp, n_tp)

    def cell(s, tt):
        return got.at[:, pl.ds(pl.multiple_of((s * n_tp + tt) * slots, 8), slots)]

    def cp_copy(d):
        peer = flip(c, d, n_cp)
        return remote(xg.at[:, peer], cell(c, t), cp_s.at[d], cp_r.at[d], (peer, t))

    def have(d):
        return xg.at[:, c] if d == 0 else cell(flip(c, d, n_cp), t)

    def y_copy(d, dy):
        to = ((y + dy) % n_y) * 2 + k
        return remote(have(d), cell(flip(c, d, n_cp), t), y_s.at[d, dy], y_r.at[d, dy], (c, to))

    def s_copy(d):
        return remote(have(d), cell(flip(c, d, n_cp), t), s_s.at[d], s_r.at[d], (c, sib))

    def f_copy(d, dy):
        part = cell(flip(c, d, n_cp), ((y + n_y - dy) % n_y) * 2 + k)
        return remote(part, part, f_s.at[d, dy], f_r.at[d, dy], (c, sib))

    def rs_copy(d, yy):
        return remote(
            p.at[d * n_tp + yy * 2 + 1 - k], a.at[d * n_y + yy],
            rs_s.at[d, yy], rs_r.at[d, yy], (c, sib),
        )

    def ry_copy(d, dy):
        to = ((y + dy) % n_y) * 2 + k
        return remote(sb.at[d, dy - 1], yb.at[d, dy - 1], ry_s.at[d, dy], ry_r.at[d, dy], (c, to))

    def rc_copy(d):
        peer = flip(c, d, n_cp)
        return remote(tb.at[d], out.at[c], rc_s.at[d], rc_r.at[d], (peer, t))

    def pair(d, yy):
        return p[d * n_tp + yy * 2 + k].astype(F32) + a[d * n_y + yy].astype(F32)

    def compute(d, slot):
        s = flip(c, d, n_cp)
        at = pl.ds(pl.multiple_of(s * rows, 16), rows)
        x = buf[slot, 0]
        gate = lax.dot_general(x, wg[...], ROWS_LAST, preferred_element_type=F32)
        upval = lax.dot_general(x, wu[...], ROWS_LAST, preferred_element_type=F32)
        gh = lax.dot_general(buf[slot, 1], wd[...], ROWS_LAST, preferred_element_type=F32)
        sig = jax.nn.sigmoid(gate)
        act = gate * sig
        gu = (gh * act).astype(BF16)
        gg = (gh * upval * sig * (1.0 + gate * (1.0 - sig))).astype(BF16)
        hid_o[at] = (act * upval).astype(BF16)
        gu_o[at] = gu
        gg_o[at] = gg
        step = 512

        def tile(i, carry):
            cols = pl.ds(pl.multiple_of(i * step, step), step)
            v = jnp.dot(gg_o[at], wg[:, cols], preferred_element_type=F32)
            v = v + jnp.dot(gu_o[at], wu[:, cols], preferred_element_type=F32)
            for tt in range(n_tp):
                p[d * n_tp + tt, :, cols] = v[tt * slots:(tt + 1) * slots].astype(BF16)
            return carry

        lax.fori_loop(0, width // step, tile, 0)

    own = pltpu.make_async_copy(xg.at[:, c], cell(c, t), loc.at[0])
    own.start()
    far = list(range(n_cp // 2, n_cp))
    near = list(range(1, n_cp // 2))
    after = {}
    for queue in (far, near):
        for j, d in enumerate(queue):
            if j < DEPTH:
                cp_copy(d).start()
            else:
                after[queue[j - DEPTH]] = d
    for copy in loads:
        copy.start()
    home = pltpu.make_async_copy(tb.at[0], out.at[c], loc.at[1])

    def chunk_load(d, slot):
        s = flip(c, d, n_cp)
        at = pl.ds(pl.multiple_of(s * rows, 16), rows)
        return pltpu.make_async_copy(got.at[:, at], buf.at[slot], l_sem.at[slot])

    order = process_order(n_cp)
    held = []
    steps = len(order)

    def chunk(i):
        return order[i] if 0 <= i < steps else None

    for i in range(steps + 4):
        d = chunk(i)
        if d is not None:
            if d:
                cp_copy(d).wait_recv()
            if d in after:
                cp_copy(d).wait_send()
                cp_copy(after[d]).start()
            if i == steps - 1:
                cp_copy(d).wait_send()
                for e in held:
                    rc_copy(e).start()
            for dy in range(1, n_y):
                y_copy(d, dy).start()
            s_copy(d).start()
        d = chunk(i - 1)
        if d is not None:
            for dy in range(1, n_y):
                y_copy(d, dy).wait_recv()
                f_copy(d, dy).start()
        d = chunk(i - 3)
        if d is not None:
            for yy in range(n_y):
                rs_copy(d, yy).wait_recv()
            for dy in range(1, n_y):
                sb[d, dy - 1] = pair(d, (y + dy) % n_y).astype(BF16)
                ry_copy(d, dy).start()
        d = chunk(i - 2)
        if d is not None:
            s_copy(d).wait_recv()
            for dy in range(1, n_y):
                f_copy(d, dy).wait_recv()
            if d == 0:
                own.wait()
            load = chunk_load(d, i % 2)
            load.start()
            if i == 2:
                for copy in loads:
                    copy.wait()
            load.wait()
            compute(d, i % 2)
            for yy in range(n_y):
                rs_copy(d, yy).start()
        d = chunk(i - 4)
        if d is not None:
            total = pair(d, y)
            for dy in range(1, n_y):
                ry_copy(d, dy).wait_recv()
                total = total + yb[d, dy - 1].astype(F32)
            tb[d] = total.astype(BF16)
            if d >= n_cp // 2 and i < steps - 1:
                held.append(d)
            elif d:
                rc_copy(d).start()
            else:
                home.start()
    home.wait()
    for d in range(n_cp):
        if d and d not in after and d != order[-1]:
            cp_copy(d).wait_send()
        if d:
            rc_copy(d).wait()
        s_copy(d).wait_send()
        for dy in range(1, n_y):
            y_copy(d, dy).wait_send()
            f_copy(d, dy).wait_send()
            ry_copy(d, dy).wait_send()
        for yy in range(n_y):
            rs_copy(d, yy).wait_send()


def fused(xg, w_gate, w_up, w_down, n_cp, n_tp):
    _, _, slots, width = xg.shape
    hid = w_gate.shape[0]
    n_y = n_tp // 2
    rows = n_tp * slots
    dma = pltpu.SemaphoreType.DMA
    anyspace = pl.BlockSpec(memory_space=pl.ANY)
    vmem = pl.BlockSpec(memory_space=pltpu.VMEM)
    one = dma((n_cp,))
    two = dma((n_cp, n_y))
    small = jax.ShapeDtypeStruct((n_cp * rows, hid), BF16)
    total = n_cp * rows
    return pl.pallas_call(
        functools.partial(fused_kernel, n_cp, n_tp, slots),
        out_shape=(
            jax.ShapeDtypeStruct((2, total, width), BF16), small, small, small,
            jax.ShapeDtypeStruct((n_cp, slots, width), BF16),
        ),
        in_specs=[anyspace] * 4,
        out_specs=(anyspace, vmem, vmem, vmem, vmem),
        scratch_shapes=[
            pltpu.VMEM((hid, width), BF16),
            pltpu.VMEM((hid, width), BF16),
            pltpu.VMEM((hid, width), BF16),
            pltpu.VMEM((2, 2, rows, width), BF16),
            pltpu.VMEM((n_cp * n_tp, slots, width), BF16),
            pltpu.VMEM((n_cp * n_y, slots, width), BF16),
            pltpu.VMEM((n_cp, n_y - 1, slots, width), BF16),
            pltpu.VMEM((n_cp, n_y - 1, slots, width), BF16),
            pltpu.VMEM((n_cp, slots, width), BF16),
            dma((2,)), dma((3,)), dma((2,)),
            one, one, two, two, one, one, two, two, two, two, two, two, one, one,
        ],
        compiler_params=pltpu.CompilerParams(
            collective_id=0, has_side_effects=True, vmem_limit_bytes=60 << 20
        ),
        cost_estimate=pl.CostEstimate(
            flops=10 * total * hid * width, bytes_accessed=8 * total * width,
            transcendentals=total * hid,
        ),
        name="fused",
    )(xg, w_gate, w_up, w_down)


def weight_kernel(xg, hid, gg, gu, d_gate, d_up, d_down, hid_t, gg_t, gu_t):
    @pl.when(pl.program_id(0) == 0)
    def _():
        hid_t[...] = hid[...].T
        gg_t[...] = gg[...].T
        gu_t[...] = gu[...].T

    x = xg[0]
    d_gate[...] = jnp.dot(gg_t[...], x, preferred_element_type=F32)
    d_up[...] = jnp.dot(gu_t[...], x, preferred_element_type=F32)
    d_down[...] = jnp.dot(hid_t[...], xg[1], preferred_element_type=F32)


def weight_grads(got, hidden, gg, gu):
    _, total, width = got.shape
    hid = hidden.shape[1]
    step = 512
    whole = pl.BlockSpec((total, hid), lambda i: (0, 0))
    grad = pl.BlockSpec((hid, step), lambda i: (0, i))
    shape = jax.ShapeDtypeStruct((hid, width), F32)
    return pl.pallas_call(
        weight_kernel,
        grid=(width // step,),
        out_shape=(shape,) * 3,
        in_specs=[pl.BlockSpec((2, total, step), lambda i: (0, 0, i)), whole, whole, whole],
        out_specs=(grad,) * 3,
        scratch_shapes=[pltpu.VMEM((hid, total), BF16)] * 3,
        compiler_params=pltpu.CompilerParams(vmem_limit_bytes=48 << 20),
        cost_estimate=pl.CostEstimate(
            flops=6 * total * hid * width, bytes_accessed=4 * total * width + 12 * hid * width,
            transcendentals=0,
        ),
        name="weight_grads",
    )(got, hidden, gg, gu)


def body(tokens, grad_out, expert_ids, router_weights, gate_weight, up_weight, down_weight):
    n_cp = lax.axis_size("cp")
    n_tp = lax.axis_size("tp")
    tok_rows, width = tokens.shape
    picks = expert_ids.shape[1]
    count = tok_rows * picks
    slots = -(-max(2, 3 * tok_rows * picks // (2 * n_cp)) // 8) * 8
    flat_ids = expert_ids.reshape(count)
    onehot = (flat_ids[:, None] == jnp.arange(n_cp, dtype=jnp.int32)[None, :]).astype(jnp.int32)
    before = jnp.cumsum(onehot, axis=0) - onehot
    rank = jnp.sum(before * onehot, axis=1)
    place = flat_ids * slots + rank
    placer = (place[None, :] == jnp.arange(n_cp * slots, dtype=jnp.int32)[:, None]).astype(BF16)
    x_assign = jnp.repeat(tokens, picks, axis=0)
    g_assign = (router_weights.reshape(count, 1) * jnp.repeat(grad_out, picks, axis=0).astype(F32)).astype(BF16)
    xg = jnp.stack([
        jnp.dot(placer, x_assign, preferred_element_type=F32).astype(BF16),
        jnp.dot(placer, g_assign, preferred_element_type=F32).astype(BF16),
    ]).reshape(2, n_cp, slots, width)
    w_gate = gate_weight[0]
    w_up = up_weight[0]
    w_down = down_weight[0]
    got, hidden, grad_gatein, grad_upin, slot_grad = fused(xg, w_gate, w_up, w_down, n_cp, n_tp)
    grad_gate, grad_up, grad_down = weight_grads(got, hidden, grad_gatein, grad_upin)
    pick_grad = lax.dot_general(
        placer, slot_grad.reshape(n_cp * slots, width), ROWS_FIRST, preferred_element_type=F32
    )
    grad_tokens = jnp.sum(pick_grad.reshape(tok_rows, picks, width), axis=1).astype(BF16)
    return (grad_tokens, grad_gate[None], grad_up[None], grad_down[None])


def solution(mesh):
    tok = P(("cp", "tp"), None)
    wgt = P("cp", "tp", None)
    return jax.shard_map(
        body,
        mesh=mesh,
        in_specs=(tok, tok, tok, tok, wgt, wgt, wgt),
        out_specs=(tok, wgt, wgt, wgt),
        check_vma=False,
    )
```
